128 devices in a mesh: row: 16 (over x, z_lo, core), rhs: 8 (over y, z_hi).
Axes of the slice: x: 4, y: 4, z: 4 (z_hi: 2, z_lo: 2; z = z_hi * 2 + z_lo), core: 2. Of those that a mesh axis runs over, the one named last changes fastest.
Arguments:
- right_sides: float32 [32768, 8192], P('row', 'rhs'), may hold values from -6 to 6
- panel_diag: float32 [2, 512, 512], replicated, as said below
- left_factor: bfloat16 [32768, 2, 512], P('row', None, 'rhs'), may hold values from -0.25 to 0.25
- right_factor: bfloat16 [32768, 2, 512], P('row', None, 'rhs'), may hold values from -0.25 to 0.25
- tile_scale: float32 [64, 2], P('row'), may hold values from 0.3 to 1.5
- tile_rank: int32 [64, 2], P('row'), may hold values from 128 to 512, as said below
Outputs:
- solved: float32 [32768, 8192], P('row', 'rhs')
The draws below stay inside these ranges and needn't reach their ends.
Inputs may be any that keep to these rules, and one draw needn't show every extreme that they name: panel_diag[k] is lower triangular with diagonal entries of 1 or more. `tile_rank`: every rank is a multiple of 128; some block has rank 512 in both panels.
All inputs are finite; a program needn't handle non-finite values.
Results may differ from the reference program's by a relative error of at most 0.0003.
Values may be sent and summed in bfloat16 or wider, within the bound.
No kernel may reach another device: no remote copies, remote signals or barrier semaphores. Data moves between devices by JAX's collectives and lax.ppermute only.
A program may use at most 128 MiB of HBM per device.

```python
import math
import jax
import jax.numpy as jnp
from jax import lax

P_SIZE = 512
RSTEP = 128
BLK_DEV = 4
NBLK = 64
ROWS = 32768
NRHS = 8192
N_ROW = 16


def draw_panel_diag(key, part):
    first_key, second_key = jax.random.split(jax.random.fold_in(key, 11))
    lower_part = jax.random.normal(first_key, (2, P_SIZE, P_SIZE), jnp.float32) * (0.8 / math.sqrt(P_SIZE))
    middle = jax.random.uniform(second_key, (2, P_SIZE), jnp.float32, 1.0, 3.0)
    return jnp.tril(lower_part, -1) + middle[:, :, None] * jnp.eye(P_SIZE, dtype=jnp.float32)[None]


def draw_tile_rank(key, part):
    first_key, second_key = jax.random.split(jax.random.fold_in(key, 23))
    levels = jax.random.randint(first_key, (NBLK, 2), 1, P_SIZE // RSTEP + 1) * RSTEP
    chosen_block = jax.random.randint(second_key, (), 0, NBLK)
    position = jnp.arange(NBLK, dtype=jnp.int32)[:, None]
    return jnp.where(position == chosen_block, P_SIZE, levels).astype(jnp.int32)


def block_levels(rng, shape, cuts, least, largest):
    gain = 1.0
    for dim, shards_of in cuts:
        steps = jax.random.uniform(jax.random.fold_in(jax.random.fold_in(rng, 6), dim), (shards_of,), jnp.float32, least / len(cuts), largest / len(cuts))
        gain = gain * jnp.repeat(jnp.exp(steps), shape[dim] // shards_of).reshape((-1,) + (1,) * (len(shape) - 1 - dim))
    return gain


def centred(own_key, dims, deviation, most, shards=(), held_as=jnp.bfloat16):
    factor_of = block_levels(own_key, dims, shards, -0.22, 0.18) if shards else 1.0
    values = jax.random.normal(own_key, dims, jnp.float32) * deviation * factor_of
    return jnp.minimum(jnp.maximum(values, -most), most).astype(held_as)


def setup_inputs(seed: int = 0) -> dict:
    splits = jax.random.split(jax.random.key(seed), 7)
    right_sides = centred(splits[0], (ROWS, NRHS), 1.0, 6.0, ((0, 16), (1, 8)), jnp.float32)
    panel_diag = draw_panel_diag(jax.random.fold_in(splits[6], 71), 0)
    left_factor = centred(splits[2], (ROWS, 2, P_SIZE), P_SIZE ** -0.5, 0.25, ((0, 16), (2, 8)))
    right_factor = centred(splits[3], (ROWS, 2, P_SIZE), P_SIZE ** -0.5, 0.25, ((0, 16), (2, 8)))
    tile_scale = jnp.clip(jnp.exp(math.log(1.5) - 1.60943787 * jax.random.uniform(splits[4], (NBLK, 2), jnp.float32) ** block_levels(splits[4], (NBLK, 2), ((0, 16),), -0.2, 0.2)), 0.3, 1.5)
    tile_rank = draw_tile_rank(jax.random.fold_in(splits[6], 71), 0)
    return {"right_sides": right_sides, "panel_diag": panel_diag, "left_factor": left_factor, "right_factor": right_factor, "tile_scale": tile_scale, "tile_rank": tile_rank}


def reference(right_sides, panel_diag, left_factor, right_factor, tile_scale, tile_rank):
    blocks = right_sides.reshape(N_ROW, BLK_DEV, P_SIZE, NRHS)
    left_all = left_factor.reshape(N_ROW, BLK_DEV, P_SIZE, 2, P_SIZE)
    right_all = right_factor.reshape(N_ROW, BLK_DEV, P_SIZE, 2, P_SIZE)
    scales = tile_scale.reshape(N_ROW, BLK_DEV, 2)
    ranks = tile_rank.reshape(N_ROW, BLK_DEV, 2)
    global_block = (jnp.arange(BLK_DEV, dtype=jnp.int32)[None, :] * N_ROW + jnp.arange(N_ROW, dtype=jnp.int32)[:, None]).astype(jnp.int32)
    columns = jnp.arange(P_SIZE, dtype=jnp.int32)
    for panel_index in range(2):
        solution = lax.linalg.triangular_solve(panel_diag[panel_index], blocks[panel_index, 0], left_side=True, lower=True)

        def update(items):
            left_block, right_block, scale_row, rank_row, global_row, target = items
            weight = jnp.where(global_row > panel_index, scale_row, 0.0).astype(jnp.float32)[:, None] * (columns[None, :] < rank_row[:, None]).astype(jnp.float32)
            inner = jnp.einsum('lqr,qn->lrn', right_block[:, :, panel_index, :].astype(jnp.float32), solution, precision=lax.Precision.HIGHEST)
            inner = inner * weight[:, :, None]
            return target - jnp.einsum('lpr,lrn->lpn', left_block[:, :, panel_index, :].astype(jnp.float32), inner, precision=lax.Precision.HIGHEST)
        blocks = lax.map(update, (left_all, right_all, scales[:, :, panel_index], ranks[:, :, panel_index], global_block, blocks))
        blocks = blocks.at[panel_index, 0].set(solution)
    return blocks.reshape(ROWS, NRHS)
```

```python
import jax
import jax.numpy as jnp
from jax import lax
from jax.experimental import pallas as pl
from jax.experimental.pallas import tpu as pltpu
from jax.sharding import PartitionSpec as P


SIZE = 512
TILE = 128
STEP = 256
BOTH = ("row", "rhs")
NX, NL, NC, NY, NH = 4, 2, 2, 4, 2
F32, BF16 = jnp.float32, jnp.bfloat16


def flat(x, low, core, y, high):
    return ((x % NX) * 4 + (low % NL) * 2 + core % NC) * 8 + (y % NY) * 2 + high % NH


def moves(shift, keep):
    pairs = []
    for x in range(NX):
        for low in range(NL):
            for core in range(NC):
                for y in range(NY):
                    for high in range(NH):
                        place = (x, low, core, y, high)
                        if keep is None or keep(*place[:3]):
                            pairs.append((flat(*place), flat(*(a + b for a, b in zip(place, shift)))))
    return pairs


def shifted(value, x=0, low=0, core=0, y=0, high=0, keep=None):
    return lax.ppermute(value, BOTH, moves((x, low, core, y, high), keep))


def dot(a, b):
    return lax.dot_general(a, b, (((1,), (0,)), ((), ())), preferred_element_type=F32)


def dot_exact(a, b):
    return lax.dot_general(
        a, b, (((1,), (0,)), ((), ())), precision=lax.Precision.HIGHEST, preferred_element_type=F32
    )


def halves(value):
    high = value.astype(BF16)
    return high, (value - high.astype(F32)).astype(BF16)


def dot_split(a, b):
    a_high, a_low = halves(a)
    b_high, b_low = halves(b)
    return dot(a_high, b_high) + (dot(a_high, b_low) + dot(a_low, b_high))


def invert_kernel(d_ref, o_ref):
    o_ref[...] = jnp.zeros_like(o_ref)
    sub = lax.broadcasted_iota(jnp.int32, (8, TILE), 0)
    row_id = lax.broadcasted_iota(jnp.int32, (TILE, TILE), 0)
    lane_id = lax.broadcasted_iota(jnp.int32, (TILE, TILE), 1)
    eye = row_id == lane_id

    def one(t, carry):
        span = pl.ds(pl.multiple_of(t * TILE, TILE), TILE)
        work = []
        for p in range(2):
            lower = d_ref[p, span, span]
            diag = jnp.where(eye, lower, 0.0)
            lanes = 1.0 / jnp.sum(diag, axis=0, keepdims=True)
            rows = 1.0 / jnp.sum(diag, axis=1, keepdims=True)
            unit = jnp.where(row_id > lane_id, lower * lanes, 0.0)
            start = eye.astype(F32)
            work.append(
                (
                    [unit[8 * b : 8 * b + 8] for b in range(16)],
                    [start[8 * b : 8 * b + 8] for b in range(16)],
                    rows,
                )
            )
        for i in range(TILE - 1):
            for unit, state, _ in work:
                row = state[i // 8][i % 8 : i % 8 + 1, :]
                for b in range((i + 1) // 8, 16):
                    state[b] = state[b] - unit[b][:, i : i + 1] * row
        for p in range(2):
            o_ref[p, span, span] = jnp.concatenate(work[p][1], axis=0) * work[p][2]
        return carry

    lax.fori_loop(0, SIZE // TILE, one, 0)
    for size in (TILE, 2 * TILE):
        for base in range(0, SIZE, 2 * size):
            for p in range(2):
                first, second = slice(base, base + size), slice(base + size, base + 2 * size)
                inner = dot_exact(d_ref[p, second, first], o_ref[p, first, first])
                o_ref[p, second, first] = -dot_exact(o_ref[p, second, second], inner)


def inverses(panel_diag):
    return pl.pallas_call(
        invert_kernel,
        out_shape=jax.ShapeDtypeStruct(panel_diag.shape, F32),
        name="inverses",
        cost_estimate=pl.CostEstimate(flops=2_000_000_000, bytes_accessed=4 << 20, transcendentals=0),
    )(panel_diag)


def first_kernel(d_ref, b_ref, x_ref):
    x_ref[...] = dot_split(d_ref[0], b_ref[...])


def first_solution(inverse, right):
    width = right.shape[1]
    return pl.pallas_call(
        first_kernel,
        grid=(width // STEP,),
        in_specs=[
            pl.BlockSpec((1, SIZE, SIZE), lambda n: (0, 0, 0)),
            pl.BlockSpec((SIZE, STEP), lambda n: (0, n)),
        ],
        out_specs=pl.BlockSpec((SIZE, STEP), lambda n: (0, n)),
        out_shape=jax.ShapeDtypeStruct(right.shape, F32),
        name="first_solution",
        cost_estimate=pl.CostEstimate(flops=1_600_000_000, bytes_accessed=5 << 20, transcendentals=0),
    )(inverse, right)


def second_kernel(coef_ref, d_ref, first_ref, b_ref, *refs):
    pieces, x_ref = refs[:-1], refs[-1]

    @pl.when(coef_ref[0, 8] > 0.0)
    def _():
        x_high, x_low = halves(dot_split(d_ref[0], first_ref[...]))
        inner_high, inner_low = [], []
        for j, piece in enumerate(pieces):
            left = jnp.concatenate([piece[64 * t : 64 * t + 64] for t in range(4)], axis=1)
            inner = (dot(left, x_high) + dot(left, x_low)) * coef_ref[0, j]
            high, low = halves(inner)
            inner_high.append(high)
            inner_low.append(low)
        stack = jnp.concatenate(
            [
                jnp.concatenate([piece[256 + 64 * t : 256 + 64 * t + 64] for t in range(4)], axis=1)
                for piece in pieces
            ],
            axis=0,
        )
        right = stack.T
        change = dot(right, jnp.concatenate(inner_high, axis=0)) + dot(right, jnp.concatenate(inner_low, axis=0))
        x_ref[...] = dot_split(d_ref[1], b_ref[...] - change)


def second_solution(coef, inverse, first, right_sides, pieces):
    width = first.shape[1]
    return pl.pallas_call(
        second_kernel,
        grid=(width // STEP,),
        in_specs=[
            pl.BlockSpec(memory_space=pltpu.SMEM),
            pl.BlockSpec((2, SIZE, SIZE), lambda n: (0, 0, 0)),
            pl.BlockSpec((SIZE, STEP), lambda n: (0, n)),
            pl.BlockSpec((SIZE, STEP), lambda n: (0, n)),
        ]
        + [pl.BlockSpec((512, TILE), lambda n: (0, 0)) for _ in pieces],
        out_specs=pl.BlockSpec((SIZE, STEP), lambda n: (0, n)),
        out_shape=jax.ShapeDtypeStruct((SIZE, width), F32),
        name="second_solution",
        cost_estimate=pl.CostEstimate(flops=4_000_000_000, bytes_accessed=9 << 20, transcendentals=0),
    )(coef, inverse, first, right_sides, *pieces)


def update_kernel(coef_ref, flag_ref, x0_ref, x1_ref, b_ref, *refs):
    blocks, (o_ref, high_ref, low_ref) = refs[:-3], refs[-3:]
    block, step = pl.program_id(0), pl.program_id(1)
    span = pl.ds(pl.multiple_of(step * STEP, STEP), STEP)

    @pl.when(block == 0)
    def _():
        for p, ref in enumerate((x0_ref, x1_ref)):
            high, low = halves(ref[:, span])
            high_ref[p, :, span] = high
            low_ref[p, :, span] = low

    whole, split = blocks[:6], blocks[6:]
    pieces = [ref[0] for ref in whole]
    for early, late in zip(split[::2], split[1::2]):
        pieces.append(jnp.where(block < 2, early[0], late[0]))

    inner_high, inner_low = [[None] * 8, [None] * 8], [[None] * 8, [None] * 8]
    for p in range(2):
        left = jnp.concatenate(
            [
                jnp.concatenate([piece[TILE * t + 64 * p : TILE * t + 64 * p + 64] for t in range(4)], axis=1)
                for piece in pieces
            ],
            axis=0,
        )
        inner = dot(left, high_ref[p, :, span]) + dot(left, low_ref[p, :, span])
        for j in range(8):
            inner_high[p][j], inner_low[p][j] = halves(
                inner[64 * j : 64 * j + 64] * coef_ref[block, 8 * p + j]
            )
    right = jnp.concatenate([piece[SIZE:] for piece in pieces], axis=1)
    stack_high = jnp.concatenate([inner_high[p][j] for j in range(8) for p in range(2)], axis=0)
    stack_low = jnp.concatenate([inner_low[p][j] for j in range(8) for p in range(2)], axis=0)
    o_ref[...] = b_ref[...] - (dot(right, stack_high) + dot(right, stack_low))

    @pl.when((block == 0) & (flag_ref[0] == 0))
    def _():
        o_ref[...] = x0_ref[:, span]

    @pl.when((block == 0) & (flag_ref[0] == 1))
    def _():
        o_ref[...] = x1_ref[:, span]


def update(coef, flag, first, second, right_sides, whole, split):
    rows, width = right_sides.shape
    count = rows // SIZE
    piece_block = (1, 2 * SIZE, TILE)
    return pl.pallas_call(
        update_kernel,
        grid=(count, width // STEP),
        in_specs=[
            pl.BlockSpec(memory_space=pltpu.SMEM),
            pl.BlockSpec(memory_space=pltpu.SMEM),
            pl.BlockSpec((SIZE, width), lambda l, n: (0, 0)),
            pl.BlockSpec((SIZE, width), lambda l, n: (0, 0)),
            pl.BlockSpec((SIZE, STEP), lambda l, n: (l, n)),
        ]
        + [pl.BlockSpec(piece_block, lambda l, n: (l, 0, 0)) for _ in whole]
        + [
            pl.BlockSpec(piece_block, (lambda l, n: (jnp.minimum(l, 1), 0, 0)) if i % 2 == 0
                         else (lambda l, n: (jnp.maximum(l - 2, 0), 0, 0)))
            for i in range(len(split))
        ],
        out_specs=pl.BlockSpec((SIZE, STEP), lambda l, n: (l, n)),
        out_shape=jax.ShapeDtypeStruct((rows, width), F32),
        scratch_shapes=[pltpu.VMEM((2, SIZE, width), BF16), pltpu.VMEM((2, SIZE, width), BF16)],
        name="update",
        cost_estimate=pl.CostEstimate(flops=17_000_000_000, bytes_accessed=30 << 20, transcendentals=0),
    )(coef, flag, first, second, right_sides, *whole, *split)


def spread(value, core, x, low, here):
    quarter = [value[TILE * k : TILE * k + TILE] for k in range(4)]
    root = lambda a, b, c: a == 0 and b == 0 and c == core
    plane = lambda a, b, c: b == 0 and c == core
    lane = lambda a, b, c: c == core
    from_root = (
        shifted(quarter[1], x=1, keep=root) + shifted(quarter[3], x=-1, keep=root) + shifted(quarter[2], x=2, keep=root)
    )
    own = jnp.where(x == 0, quarter[0], from_root)
    own = jnp.where(low == 0, own, shifted(own, low=1, keep=plane))
    after = shifted(own, x=-1, keep=lane)
    before = shifted(own, x=1, keep=lane)
    across = shifted(own, x=2, keep=lane)
    ring = [own, after, across, before]
    parts = [
        jnp.where(x == k, ring[0], jnp.where(x == (k - 1) % 4, ring[1], jnp.where(x == (k - 2) % 4, ring[2], ring[3])))
        for k in range(4)
    ]
    full = jnp.concatenate(parts, axis=0)
    return jnp.where(here == core, full, shifted(full, core=1, keep=lane))


def shards(right_sides, panel_diag, left_factor, right_factor, tile_scale, tile_rank):
    rows, width = right_sides.shape
    count = rows // SIZE
    row = lax.axis_index("row")
    col = lax.axis_index("rhs")
    x, low, core = row // 4, (row // 2) % 2, row % 2
    y, high = col // 2, col % 2

    left_lanes = jnp.transpose(right_factor, (1, 2, 0)).reshape(TILE, count, 4, TILE)
    left_lanes = jnp.transpose(left_lanes, (1, 2, 0, 3)).reshape(count, SIZE, TILE)
    packed = jnp.concatenate([left_lanes, left_factor.reshape(count, SIZE, TILE)], axis=1)

    def lone(factor):
        return jnp.transpose(
            jnp.transpose(factor[:SIZE, 0, :], (1, 0)).reshape(64, 4, TILE), (1, 0, 2)
        ).reshape(256, TILE)

    tile = jnp.concatenate([lone(right_factor), lone(left_factor)], axis=0)
    solver = lambda a, b, c: a == 0 and b == 0 and c == 1
    order = [(0, 0)] + [(dy, dh) for dh in (0, 1) for dy in (1, 3, 2) if (dy, dh) != (0, 0)] + [(0, 1)]
    tiles = [tile] + [shifted(tile, y=dy, high=dh, keep=solver) for dy, dh in order[1:]]
    right_first = shifted(right_sides[:SIZE], core=1, keep=lambda a, b, c: a == 0 and b == 0 and c == 0)

    first_right = spread(right_sides[:SIZE], 0, x, low, core)

    up = shifted(packed, y=1)
    down = shifted(packed, y=-1)
    over = shifted(packed, high=1)
    far_early = shifted(up[:2], y=1)
    far_late = shifted(down[2:], y=-1)
    over_up = shifted(over, y=1)
    over_down = shifted(over, y=-1)
    over_far_early = shifted(far_early, high=1)
    over_far_late = shifted(far_late, high=1)
    whole = [packed, up, down, over, over_up, over_down]
    split = [far_early, far_late, over_far_early, over_far_late]
    places = [(0, 0), (-1, 0), (1, 0), (0, 1), (-1, 1), (1, 1), (2, 0), (2, 1)]

    global_block = jnp.arange(count, dtype=jnp.int32) * lax.axis_size("row") + row

    def weights(where):
        shard = jnp.stack([((y + dy) % NY) * 2 + (high + dh) % NH for dy, dh in where]).astype(jnp.int32)
        panel = jnp.arange(2, dtype=jnp.int32)
        active = jnp.where(global_block[:, None] > panel[None, :], tile_scale, 0.0)
        live = (shard * 64)[None, None, :] < tile_rank[:, :, None]
        return jnp.where(live, active[:, :, None], 0.0).astype(F32)

    inverse = inverses(panel_diag)
    own_weights = weights([(-dy, -dh) for dy, dh in order])[:1, 0, :]
    solver_flag = jnp.where(row == 1, 1.0, 0.0).astype(F32).reshape(1, 1)
    second_local = second_solution(
        jnp.concatenate([own_weights, solver_flag], axis=1), inverse, right_first, right_sides, tiles
    )
    first = first_solution(inverse, first_right)
    second = spread(second_local, 1, x, low, core)
    coef = weights(places).reshape(count, 16)
    flag = row.astype(jnp.int32).reshape(1)
    return update(coef, flag, first, second, right_sides, whole, split)


def solution(mesh):
    placed = (
        P("row", "rhs"),
        P(),
        P("row", None, "rhs"),
        P("row", None, "rhs"),
        P("row", None),
        P("row", None),
    )
    return jax.shard_map(shards, mesh=mesh, in_specs=placed, out_specs=P("row", "rhs"), check_vma=False)
```

```python
import functools

import jax
import jax.numpy as jnp
from jax import lax
from jax.experimental import pallas as pl
from jax.experimental.pallas import tpu as pltpu
from jax.sharding import PartitionSpec as P


SIZE = 512
TILE = 128
HALF = 64
STEP = 512
BOTH = ("row", "rhs")
NX, NL, NC, NY, NH = 4, 2, 2, 4, 2
F32, BF16 = jnp.float32, jnp.bfloat16


def flat(x, low, core, y, high):
    return ((x % NX) * 4 + (low % NL) * 2 + core % NC) * 8 + (y % NY) * 2 + high % NH


def moves(shift, keep):
    pairs = []
    for x in range(NX):
        for low in range(NL):
            for core in range(NC):
                for y in range(NY):
                    for high in range(NH):
                        place = (x, low, core, y, high)
                        if keep is None or keep(*place[:3]):
                            pairs.append((flat(*place), flat(*(a + b for a, b in zip(place, shift)))))
    return pairs


def shifted(value, x=0, low=0, core=0, y=0, high=0, keep=None):
    return lax.ppermute(value, BOTH, moves((x, low, core, y, high), keep))


def dot(a, b):
    return lax.dot_general(a, b, (((1,), (0,)), ((), ())), preferred_element_type=F32)


def dot_exact(a, b):
    return lax.dot_general(
        a, b, (((1,), (0,)), ((), ())), precision=lax.Precision.HIGHEST, preferred_element_type=F32
    )


def halves(value):
    high = value.astype(BF16)
    return high, (value - high.astype(F32)).astype(BF16)


def dot_split(a, b):
    a_high, a_low = halves(a)
    b_high, b_low = halves(b)
    return dot(a_high, b_high) + (dot(a_high, b_low) + dot(a_low, b_high))


def weight(place_ref, scale_ref, rank_ref, block, panel, shift):
    shard = lax.rem(place_ref[3] + shift[0], NY) * 2 + lax.rem(place_ref[4] + shift[1], NH)
    live = (block * (NX * NL * NC) + place_ref[5] > panel) & (shard * 64 < rank_ref[panel, block])
    return jnp.where(live, scale_ref[panel, block], 0.0)


SCALARS = pl.BlockSpec(memory_space=pltpu.SMEM)
PARAMS = pltpu.CompilerParams(vmem_limit_bytes=67_043_328)


def invert_kernel(d_ref, o_ref):
    o_ref[...] = jnp.zeros_like(o_ref)
    row = lax.broadcasted_iota(jnp.int32, (HALF, TILE), 0)
    lane = lax.broadcasted_iota(jnp.int32, (HALF, TILE), 1)
    left, col = lane < HALF, lane % HALF
    left_rows = lax.broadcasted_iota(jnp.int32, (8, TILE), 1) < HALF
    tile_row = lax.broadcasted_iota(jnp.int32, (TILE, TILE), 0)
    tile_lane = lax.broadcasted_iota(jnp.int32, (TILE, TILE), 1)
    work = []
    for t in range(SIZE // TILE):
        for p in range(2):
            span = slice(t * TILE, t * TILE + TILE)
            lower = d_ref[p, span, span]
            both = jnp.where(left, lower[:HALF], lower[HALF:])
            lanes = 1.0 / jnp.sum(jnp.where(row == col, both, 0.0), axis=0, keepdims=True)
            rows = 1.0 / jnp.sum(jnp.where(tile_row == tile_lane, lower, 0.0), axis=1, keepdims=True)
            unit = jnp.where(row > col, both * lanes, 0.0)
            start = jnp.where(row == col, 1.0, 0.0).astype(F32)
            strips = range(0, HALF, 8)
            work.append((p, span, rows, [unit[b : b + 8] for b in strips], [start[b : b + 8] for b in strips]))
    for i in range(HALF - 1):
        for _, _, _, unit, state in work:
            pivot = state[i // 8][i % 8 : i % 8 + 1, :]
            for b in range((i + 1) // 8, HALF // 8):
                column = jnp.where(left_rows, unit[b][:, i : i + 1], unit[b][:, HALF + i : HALF + i + 1])
                state[b] = state[b] - column * pivot
    for p, span, rows, _, state in work:
        both = jnp.concatenate(state, axis=0)
        inverse = jnp.concatenate([jnp.where(left, both, 0.0), jnp.where(left, 0.0, both)], axis=0) * rows
        below = jnp.where((tile_row >= HALF) & (tile_lane < HALF), d_ref[p, span, span], 0.0)
        o_ref[p, span, span] = inverse - dot_exact(inverse, dot_exact(below, inverse))
    for size in (TILE, 2 * TILE):
        for base in range(0, SIZE, 2 * size):
            for p in range(2):
                first, second = slice(base, base + size), slice(base + size, base + 2 * size)
                inner = dot_exact(d_ref[p, second, first], o_ref[p, first, first])
                o_ref[p, second, first] = -dot_exact(o_ref[p, second, second], inner)


def inverses(panel_diag):
    return pl.pallas_call(
        invert_kernel,
        out_shape=jax.ShapeDtypeStruct(panel_diag.shape, F32),
        name="inverses",
        compiler_params=PARAMS,
        cost_estimate=pl.CostEstimate(flops=2_000_000_000, bytes_accessed=4 << 20, transcendentals=0),
    )(panel_diag)


def ring_rows(place_ref, k):
    return pl.ds(pl.multiple_of(lax.rem(place_ref[0] + k, 4) * TILE, TILE), TILE)


def first_kernel(place_ref, inverse, *refs):
    quarters, o_ref, d_ref, right_ref, x_ref, sems = refs[:4], *refs[4:]

    @pl.when(place_ref[2] == 0)
    def _():
        loads = [pltpu.make_async_copy(inverse.at[0], d_ref, sems.at[4])]
        for k in range(4):
            loads.append(pltpu.make_async_copy(quarters[k], right_ref.at[ring_rows(place_ref, k)], sems.at[k]))
        for load in loads:
            load.start()
        for load in loads:
            load.wait()
        x_ref[...] = dot_split(d_ref[...], right_ref[...])
        store = pltpu.make_async_copy(x_ref, o_ref, sems.at[5])
        store.start()
        store.wait()


def first_solution(place, inverse, quarters):
    width = quarters[0].shape[1]
    there = pl.BlockSpec(memory_space=pltpu.HBM)
    return pl.pallas_call(
        first_kernel,
        in_specs=[SCALARS] + [there] * 5,
        out_specs=there,
        out_shape=jax.ShapeDtypeStruct((SIZE, width), F32),
        scratch_shapes=[
            pltpu.VMEM((SIZE, SIZE), F32),
            pltpu.VMEM((SIZE, width), F32),
            pltpu.VMEM((SIZE, width), F32),
            pltpu.SemaphoreType.DMA((6,)),
        ],
        name="first_solution",
        compiler_params=PARAMS,
        cost_estimate=pl.CostEstimate(flops=1_600_000_000, bytes_accessed=5 << 20, transcendentals=0),
    )(place, inverse, *quarters)


def place_kernel(place_ref, *refs):
    quarters, o_ref, buffer, sems = refs[:4], refs[4], refs[5], refs[6]

    @pl.when(place_ref[2] == 1)
    def _():
        loads, stores = [], []
        for k in range(4):
            loads.append(pltpu.make_async_copy(quarters[k], buffer.at[k], sems.at[k]))
            stores.append(pltpu.make_async_copy(buffer.at[k], o_ref.at[ring_rows(place_ref, k)], sems.at[4 + k]))
        for load in loads:
            load.start()
        for load, store in zip(loads, stores):
            load.wait()
            store.start()
        for store in stores:
            store.wait()


def put_in_place(place, quarters):
    width = quarters[0].shape[1]
    there = pl.BlockSpec(memory_space=pltpu.HBM)
    return pl.pallas_call(
        place_kernel,
        in_specs=[SCALARS] + [there] * 4,
        out_specs=there,
        out_shape=jax.ShapeDtypeStruct((SIZE, width), F32),
        scratch_shapes=[pltpu.VMEM((4, TILE, width), F32), pltpu.SemaphoreType.DMA((8,))],
        name="placed",
        compiler_params=PARAMS,
        cost_estimate=pl.CostEstimate(flops=0, bytes_accessed=4 << 20, transcendentals=0),
    )(place, *quarters)


def second_kernel(shifts, place_ref, scale_ref, rank_ref, d_ref, b_ref, *refs):
    near, pieces, outs = refs[:4], refs[4:-4], refs[-4:]

    @pl.when(place_ref[5] == 1)
    def _():
        first = jnp.concatenate([quarter[...] for quarter in near], axis=0)
        x_high, x_low = halves(dot_split(d_ref[0], first))
        parts = [piece[SIZE * h : SIZE * h + SIZE] for piece in pieces for h in range(2)]
        wide = lambda part, base: jnp.concatenate([part[base + 64 * t : base + 64 * t + 64] for t in range(4)], axis=1)
        left = jnp.concatenate([wide(part, 0) for part in parts], axis=0)
        inner = dot(left, x_high) + dot(left, x_low)
        scaled = [
            halves(inner[64 * j : 64 * j + 64] * weight(place_ref, scale_ref, rank_ref, 0, 0, shifts[j]))
            for j in range(8)
        ]
        right = jnp.concatenate([wide(part, 256) for part in parts], axis=0).T
        change = dot(right, jnp.concatenate([high for high, _ in scaled], axis=0)) + dot(
            right, jnp.concatenate([low for _, low in scaled], axis=0)
        )
        solved = dot_split(d_ref[1], b_ref[...] - change)
        for k in range(4):
            outs[k][...] = solved[TILE * k : TILE * k + TILE]


def second_solution(scalars, shifts, inverse, near, right_sides, pieces):
    width = right_sides.shape[1]
    quarter = pl.BlockSpec((TILE, STEP), lambda n: (0, n))
    return pl.pallas_call(
        functools.partial(second_kernel, shifts),
        grid=(width // STEP,),
        in_specs=[SCALARS] * 3
        + [
            pl.BlockSpec((2, SIZE, SIZE), lambda n: (0, 0, 0)),
            pl.BlockSpec((SIZE, STEP), lambda n: (0, n)),
        ]
        + [quarter] * 4
        + [pl.BlockSpec((2 * SIZE, TILE), lambda n: (0, 0)) for _ in pieces],
        out_specs=[quarter] * 4,
        out_shape=[jax.ShapeDtypeStruct((TILE, width), F32)] * 4,
        name="second_solution",
        compiler_params=PARAMS,
        cost_estimate=pl.CostEstimate(flops=4_000_000_000, bytes_accessed=9 << 20, transcendentals=0),
    )(*scalars, inverse, right_sides, *near, *pieces)


def update_kernel(panel, shifts, place_ref, scale_ref, rank_ref, b_ref, *refs):
    blocks, rest = refs[:8], refs[8:]
    sources, (o_ref, x_ref, high_ref, low_ref, sem) = rest[:-5], rest[-5:]
    block = pl.program_id(0)
    core, row = place_ref[2], place_ref[5]
    chosen = [core == panel, core == 1 - panel]

    @pl.when(block == 0)
    def _():
        for test, source in zip(chosen, sources):

            @pl.when(test)
            def _():
                copy = pltpu.make_async_copy(source, x_ref, sem)
                copy.start()
                copy.wait()

        high, rest = halves(x_ref[...])
        high_ref[...] = high
        low_ref[...] = rest

    @pl.when((block == 0) & (row == panel))
    def _():
        o_ref[...] = x_ref[...]

    @pl.when((block == 0) & (row == 1 - panel))
    def _():
        o_ref[...] = b_ref[...]

    @pl.when((block > 0) | (row > 1))
    def _():
        pieces = [ref[0] for ref in blocks]
        base = HALF * panel
        left = jnp.concatenate(
            [
                jnp.concatenate([piece[TILE * t + base : TILE * t + base + HALF] for t in range(4)], axis=1)
                for piece in pieces
            ],
            axis=0,
        )
        inner = dot(left, high_ref[...]) + dot(left, low_ref[...])
        scaled = [
            halves(
                inner[HALF * j : HALF * j + HALF] * weight(place_ref, scale_ref, rank_ref, block, panel, shifts[j])
            )
            for j in range(8)
        ]
        right = jnp.concatenate([piece[SIZE:, base : base + HALF] for piece in pieces], axis=1)
        change = [dot(right, jnp.concatenate([pair[part] for pair in scaled], axis=0)) for part in range(2)]
        o_ref[...] = b_ref[...] - (change[0] + change[1])


def update(panel, scalars, shifts, current, pieces, sources):
    rows, width = current.shape
    part = pl.BlockSpec((SIZE, width), lambda l: (l, 0))
    return pl.pallas_call(
        functools.partial(update_kernel, panel, shifts),
        grid=(rows // SIZE,),
        in_specs=[SCALARS] * 3
        + [part]
        + [pl.BlockSpec((1, 2 * SIZE, TILE), lambda l: (l, 0, 0)) for _ in pieces]
        + [pl.BlockSpec(memory_space=pltpu.HBM) for _ in sources],
        out_specs=part,
        out_shape=jax.ShapeDtypeStruct((rows, width), F32),
        scratch_shapes=[
            pltpu.VMEM((SIZE, width), F32),
            pltpu.VMEM((SIZE, width), BF16),
            pltpu.VMEM((SIZE, width), BF16),
            pltpu.SemaphoreType.DMA(()),
        ],
        compiler_params=PARAMS,
        cost_estimate=pl.CostEstimate(flops=9_000_000_000, bytes_accessed=28 << 20, transcendentals=0),
    )(*scalars, current, *pieces, *sources)


def spread(side, quarter, x, low):
    root = lambda a, b, c: a == 0 and b == 0 and c == side
    plane = lambda a, b, c: b == 0 and c == side
    lane = lambda a, b, c: c == side
    from_root = (
        shifted(quarter[1], x=1, keep=root)
        + shifted(quarter[3], x=-1, keep=root)
        + shifted(quarter[2], x=2, keep=root)
    )
    own = jnp.where(x == 0, quarter[0], from_root)
    own = jnp.where(low == 0, own, shifted(own, low=1, keep=plane))
    after = shifted(own, x=-1, keep=lane)
    before = shifted(own, x=1, keep=lane)
    across = shifted(own, x=2, keep=lane)
    return [own, after, across, before]


def shards(right_sides, panel_diag, left_factor, right_factor, tile_scale, tile_rank):
    rows, _ = right_sides.shape
    count = rows // SIZE
    row = lax.axis_index("row")
    col = lax.axis_index("rhs")
    x, low, core = row // 4, (row // 2) % 2, row % 2
    y, high = col // 2, col % 2
    place = jnp.stack([x, low, core, y, high, row]).astype(jnp.int32)

    left_lanes = jnp.transpose(right_factor, (1, 2, 0)).reshape(TILE, count, 4, TILE)
    left_lanes = jnp.transpose(left_lanes, (1, 2, 0, 3)).reshape(count, SIZE, TILE)
    packed = jnp.concatenate([left_lanes, left_factor.reshape(count, SIZE, TILE)], axis=1)

    def lone(factor):
        return jnp.transpose(
            jnp.transpose(factor[:SIZE, 0, :], (1, 0)).reshape(64, 4, TILE), (1, 0, 2)
        ).reshape(256, TILE)

    tile = jnp.concatenate([lone(right_factor), lone(left_factor)], axis=0)
    solver = lambda a, b, c: a == 0 and b == 0 and c == 1
    tile = jnp.concatenate([tile, shifted(tile, high=1, keep=solver)], axis=0)
    turns = (1, 3, 2)
    tiles = [tile] + [shifted(tile, y=dy, keep=solver) for dy in turns]
    tile_places = [((4 - dy) % 4, dh) for dy in (0, *turns) for dh in (0, 1)]

    up = shifted(packed, y=1)
    down = shifted(packed, y=-1)
    over = shifted(packed, high=1)
    over_up = shifted(over, y=1)
    over_down = shifted(over, y=-1)
    far = shifted(up, y=1)
    over_far = shifted(over_down, y=-1)
    pieces = [packed, up, down, over, over_up, over_down, far, over_far]
    places = [(0, 0), (3, 0), (1, 0), (0, 1), (3, 1), (1, 1), (2, 0), (2, 1)]

    right = [right_sides[TILE * k : TILE * k + TILE] for k in range(4)]
    near = [shifted(quarter, core=1, keep=lambda a, b, c: a == 0 and b == 0 and c == 0) for quarter in right]
    inverse = inverses(panel_diag)
    scalars = (place, tile_scale.T, tile_rank.T)
    first = first_solution(place, inverse, spread(0, right, x, low))
    first_core = shifted(first, core=1)
    middle = update(0, scalars, places, right_sides, pieces, [first, first_core])
    quarters = second_solution(scalars, tile_places, inverse, near, right_sides, tiles)
    second = put_in_place(place, spread(1, quarters, x, low))
    second_core = shifted(second, core=1)
    return update(1, scalars, places, middle, pieces, [second, second_core])


def solution(mesh):
    placed = (
        P("row", "rhs"),
        P(),
        P("row", None, "rhs"),
        P("row", None, "rhs"),
        P("row", None),
        P("row", None),
    )
    return jax.shard_map(shards, mesh=mesh, in_specs=placed, out_specs=P("row", "rhs"), check_vma=False)
```

```python
import functools

import jax
import jax.numpy as jnp
from jax import lax
from jax.experimental import pallas as pl
from jax.experimental.pallas import tpu as pltpu
from jax.sharding import PartitionSpec as P


SIZE = 512
TILE = 128
HALF = 64
BASE = 32
STEP = 512
BOTH = ("row", "rhs")
NX, NL, NC, NY, NH = 4, 2, 2, 4, 2
F32, BF16 = jnp.float32, jnp.bfloat16


def flat(x, low, core, y, high):
    return ((x % NX) * 4 + (low % NL) * 2 + core % NC) * 8 + (y % NY) * 2 + high % NH


def moves(shift, keep):
    pairs = []
    for x in range(NX):
        for low in range(NL):
            for core in range(NC):
                for y in range(NY):
                    for high in range(NH):
                        place = (x, low, core, y, high)
                        if keep is None or keep(*place[:3]):
                            pairs.append((flat(*place), flat(*(a + b for a, b in zip(place, shift)))))
    return pairs


def shifted(value, x=0, low=0, core=0, y=0, high=0, keep=None):
    return lax.ppermute(value, BOTH, moves((x, low, core, y, high), keep))


def dot(a, b):
    return lax.dot_general(a, b, (((1,), (0,)), ((), ())), preferred_element_type=F32)


def dot_exact(a, b):
    return lax.dot_general(
        a, b, (((1,), (0,)), ((), ())), precision=lax.Precision.HIGHEST, preferred_element_type=F32
    )


def halves(value):
    high = value.astype(BF16)
    return high, (value - high.astype(F32)).astype(BF16)


def dot_split(a, b):
    a_high, a_low = halves(a)
    b_high, b_low = halves(b)
    return dot(a_high, b_high) + (dot(a_high, b_low) + dot(a_low, b_high))


def weight(place_ref, scale_ref, rank_ref, block, panel, shift):
    shard = lax.rem(place_ref[3] + shift[0], NY) * 2 + lax.rem(place_ref[4] + shift[1], NH)
    live = (block * (NX * NL * NC) + place_ref[5] > panel) & (shard * 64 < rank_ref[panel, block])
    return jnp.where(live, scale_ref[panel, block], 0.0)


SCALARS = pl.BlockSpec(memory_space=pltpu.SMEM)


def params(mib):
    return pltpu.CompilerParams(vmem_limit_bytes=mib << 20)


def invert_kernel(d_ref, o_ref):
    o_ref[...] = jnp.zeros_like(o_ref)
    row = lax.broadcasted_iota(jnp.int32, (BASE, TILE), 0)
    lane = lax.broadcasted_iota(jnp.int32, (BASE, TILE), 1)
    part, col = lane // BASE, lane % BASE
    part_rows = lax.broadcasted_iota(jnp.int32, (8, TILE), 1) // BASE
    tile_row = lax.broadcasted_iota(jnp.int32, (TILE, TILE), 0)
    tile_lane = lax.broadcasted_iota(jnp.int32, (TILE, TILE), 1)
    pick = lambda at, values: jnp.where(
        at < 2, jnp.where(at == 0, values[0], values[1]), jnp.where(at == 2, values[2], values[3])
    )
    work = []
    for t in range(SIZE // TILE):
        for p in range(2):
            span = slice(t * TILE, t * TILE + TILE)
            lower = d_ref[p, span, span]
            packed = pick(part, [lower[BASE * k : BASE * k + BASE] for k in range(4)])
            lanes = 1.0 / jnp.sum(jnp.where(row == col, packed, 0.0), axis=0, keepdims=True)
            rows = 1.0 / jnp.sum(jnp.where(tile_row == tile_lane, lower, 0.0), axis=1, keepdims=True)
            unit = jnp.where(row > col, packed * lanes, 0.0)
            start = jnp.where(row == col, 1.0, 0.0).astype(F32)
            strips = range(0, BASE, 8)
            work.append((p, span, rows, [unit[b : b + 8] for b in strips], [start[b : b + 8] for b in strips]))
    for i in range(BASE - 1):
        for _, _, _, unit, state in work:
            pivot = state[i // 8][i % 8 : i % 8 + 1, :]
            for b in range((i + 1) // 8, BASE // 8):
                column = pick(part_rows, [unit[b][:, BASE * k + i : BASE * k + i + 1] for k in range(4)])
                state[b] = state[b] - column * pivot
    for p, span, rows, _, state in work:
        packed = jnp.concatenate(state, axis=0)
        inverse = jnp.concatenate([jnp.where(part == k, packed, 0.0) for k in range(4)], axis=0) * rows
        for size in (BASE, 2 * BASE):
            pair = (tile_row // size == tile_lane // size + 1) & (tile_lane // size % 2 == 0)
            below = jnp.where(pair, d_ref[p, span, span], 0.0)
            inverse = inverse - dot_exact(inverse, dot_exact(below, inverse))
        o_ref[p, span, span] = inverse
    for size in (TILE, 2 * TILE):
        for base in range(0, SIZE, 2 * size):
            for p in range(2):
                first, second = slice(base, base + size), slice(base + size, base + 2 * size)
                inner = dot_exact(d_ref[p, second, first], o_ref[p, first, first])
                o_ref[p, second, first] = -dot_exact(o_ref[p, second, second], inner)


def inverses(panel_diag):
    return pl.pallas_call(
        invert_kernel,
        out_shape=jax.ShapeDtypeStruct(panel_diag.shape, F32),
        name="inverses",
        compiler_params=params(28),
        cost_estimate=pl.CostEstimate(flops=2_000_000_000, bytes_accessed=4 << 20, transcendentals=0),
    )(panel_diag)


def root_kernel(place_ref, source, *refs):
    outs, buffer, sems = refs[:5], refs[5], refs[6]

    @pl.when(place_ref[5] == 0)
    def _():
        rows = lambda k: pl.ds(k * TILE, TILE)
        loads = [pltpu.make_async_copy(source.at[rows(k)], buffer.at[rows(k)], sems.at[k]) for k in range(4)]
        stores = [pltpu.make_async_copy(buffer.at[rows(k)], outs[k], sems.at[4 + k]) for k in range(4)]
        whole = pltpu.make_async_copy(buffer, outs[4], sems.at[8])
        for load in loads:
            load.start()
        for load, store in zip(loads, stores):
            load.wait()
            store.start()
        whole.start()
        for store in stores:
            store.wait()
        whole.wait()


def root_copies(place, right_sides):
    width = right_sides.shape[1]
    there = pl.BlockSpec(memory_space=pltpu.HBM)
    quarter = jax.ShapeDtypeStruct((TILE, width), F32)
    return pl.pallas_call(
        root_kernel,
        in_specs=[SCALARS, there],
        out_specs=[there] * 5,
        out_shape=[quarter] * 4 + [jax.ShapeDtypeStruct((SIZE, width), F32)],
        scratch_shapes=[pltpu.VMEM((SIZE, width), F32), pltpu.SemaphoreType.DMA((9,))],
        name="root_copies",
        compiler_params=params(63),
        cost_estimate=pl.CostEstimate(flops=0, bytes_accessed=6 << 20, transcendentals=0),
    )(place, right_sides)


def ring_rows(place_ref, k):
    return pl.ds(pl.multiple_of(lax.rem(place_ref[0] + k, 4) * TILE, TILE), TILE)


def first_kernel(place_ref, inverse, *refs):
    quarters, o_ref, d_ref, right_ref, x_ref, sems = refs[:4], *refs[4:]

    @pl.when(place_ref[2] == 0)
    def _():
        loads = [pltpu.make_async_copy(inverse.at[0], d_ref, sems.at[4])]
        for k in range(4):
            loads.append(pltpu.make_async_copy(quarters[k], right_ref.at[ring_rows(place_ref, k)], sems.at[k]))
        for load in loads:
            load.start()
        for load in loads:
            load.wait()
        x_ref[...] = dot_split(d_ref[...], right_ref[...])
        store = pltpu.make_async_copy(x_ref, o_ref, sems.at[5])
        store.start()
        store.wait()


def first_solution(place, inverse, quarters):
    width = quarters[0].shape[1]
    there = pl.BlockSpec(memory_space=pltpu.HBM)
    return pl.pallas_call(
        first_kernel,
        in_specs=[SCALARS] + [there] * 5,
        out_specs=there,
        out_shape=jax.ShapeDtypeStruct((SIZE, width), F32),
        scratch_shapes=[
            pltpu.VMEM((SIZE, SIZE), F32),
            pltpu.VMEM((SIZE, width), F32),
            pltpu.VMEM((SIZE, width), F32),
            pltpu.SemaphoreType.DMA((6,)),
        ],
        name="first_solution",
        compiler_params=params(28),
        cost_estimate=pl.CostEstimate(flops=1_600_000_000, bytes_accessed=5 << 20, transcendentals=0),
    )(place, inverse, *quarters)


def second_kernel(shifts, place_ref, scale_ref, rank_ref, d_ref, b_ref, near_ref, *refs):
    pieces, outs = refs[:-4], refs[-4:]

    @pl.when(place_ref[5] == 1)
    def _():
        x_high, x_low = halves(dot_split(d_ref[0], near_ref[...]))
        parts = [piece[SIZE * h : SIZE * h + SIZE] for piece in pieces for h in range(2)]
        wide = lambda part, base: jnp.concatenate([part[base + 64 * t : base + 64 * t + 64] for t in range(4)], axis=1)
        left = jnp.concatenate([wide(part, 0) for part in parts], axis=0)
        inner = dot(left, x_high) + dot(left, x_low)
        scaled = [
            halves(inner[64 * j : 64 * j + 64] * weight(place_ref, scale_ref, rank_ref, 0, 0, shifts[j]))
            for j in range(8)
        ]
        right = jnp.concatenate([wide(part, 256) for part in parts], axis=0).T
        change = dot(right, jnp.concatenate([high for high, _ in scaled], axis=0)) + dot(
            right, jnp.concatenate([low for _, low in scaled], axis=0)
        )
        solved = dot_split(d_ref[1], b_ref[...] - change)
        for k in range(4):
            outs[k][...] = solved[TILE * k : TILE * k + TILE]


def second_solution(scalars, shifts, inverse, near, right_sides, pieces):
    width = right_sides.shape[1]
    quarter = pl.BlockSpec((TILE, STEP), lambda n: (0, n))
    return pl.pallas_call(
        functools.partial(second_kernel, shifts),
        grid=(width // STEP,),
        in_specs=[SCALARS] * 3
        + [
            pl.BlockSpec((2, SIZE, SIZE), lambda n: (0, 0, 0)),
            pl.BlockSpec((SIZE, STEP), lambda n: (0, n)),
            pl.BlockSpec((SIZE, STEP), lambda n: (0, n)),
        ]
        + [pl.BlockSpec((2 * SIZE, TILE), lambda n: (0, 0)) for _ in pieces],
        out_specs=[quarter] * 4,
        out_shape=[jax.ShapeDtypeStruct((TILE, width), F32)] * 4,
        name="second_solution",
        compiler_params=params(44),
        cost_estimate=pl.CostEstimate(flops=4_000_000_000, bytes_accessed=9 << 20, transcendentals=0),
    )(*scalars, inverse, right_sides, near, *pieces)


def update_kernel(panel, shifts, place_ref, scale_ref, rank_ref, b_ref, *refs):
    blocks, rest = refs[:8], refs[8:]
    sources, (o_ref, x_ref, high_ref, low_ref, sem) = rest[:-5], rest[-5:]
    block = pl.program_id(0)
    core, row = place_ref[2], place_ref[5]
    count = len(sources) // 2

    @pl.when(block == 0)
    def _():
        for test, parts in ((core == panel, sources[:count]), (core != panel, sources[count:])):

            @pl.when(test)
            def _():
                copies = []
                for k, part in enumerate(parts):
                    there = x_ref if count == 1 else x_ref.at[ring_rows(place_ref, k)]
                    copies.append(pltpu.make_async_copy(part, there, sem.at[k]))
                for copy in copies:
                    copy.start()
                for copy in copies:
                    copy.wait()

        high, rest = halves(x_ref[...])
        high_ref[...] = high
        low_ref[...] = rest

    @pl.when((block == 0) & (row == panel))
    def _():
        o_ref[...] = x_ref[...]

    @pl.when((block == 0) & (row == 1 - panel))
    def _():
        o_ref[...] = b_ref[...]

    @pl.when((block > 0) | (row > 1))
    def _():
        pieces = [ref[0] for ref in blocks]
        base = HALF * panel
        left = jnp.concatenate(
            [
                jnp.concatenate([piece[TILE * t + base : TILE * t + base + HALF] for t in range(4)], axis=1)
                for piece in pieces
            ],
            axis=0,
        )
        inner = dot(left, high_ref[...]) + dot(left, low_ref[...])
        scaled = [
            halves(
                inner[HALF * j : HALF * j + HALF] * weight(place_ref, scale_ref, rank_ref, block, panel, shifts[j])
            )
            for j in range(8)
        ]
        right = jnp.concatenate([piece[SIZE:, base : base + HALF] for piece in pieces], axis=1)
        change = [dot(right, jnp.concatenate([pair[part] for pair in scaled], axis=0)) for part in range(2)]
        o_ref[...] = b_ref[...] - (change[0] + change[1])


def update(panel, scalars, shifts, current, pieces, sources):
    rows, width = current.shape
    part = pl.BlockSpec((SIZE, width), lambda l: (l, 0))
    return pl.pallas_call(
        functools.partial(update_kernel, panel, shifts),
        grid=(rows // SIZE,),
        in_specs=[SCALARS] * 3
        + [part]
        + [pl.BlockSpec((1, 2 * SIZE, TILE), lambda l: (l, 0, 0)) for _ in pieces]
        + [pl.BlockSpec(memory_space=pltpu.HBM) for _ in sources],
        out_specs=part,
        out_shape=jax.ShapeDtypeStruct((rows, width), F32),
        scratch_shapes=[
            pltpu.VMEM((SIZE, width), F32),
            pltpu.VMEM((SIZE, width), BF16),
            pltpu.VMEM((SIZE, width), BF16),
            pltpu.SemaphoreType.DMA((4,)),
        ],
        compiler_params=params(28),
        cost_estimate=pl.CostEstimate(flops=9_000_000_000, bytes_accessed=28 << 20, transcendentals=0),
    )(*scalars, current, *pieces, *sources)


def spread(side, quarter, x, low):
    root = lambda a, b, c: a == 0 and b == 0 and c == side
    plane = lambda a, b, c: b == 0 and c == side
    lane = lambda a, b, c: c == side
    from_root = (
        shifted(quarter[1], x=1, keep=root)
        + shifted(quarter[3], x=-1, keep=root)
        + shifted(quarter[2], x=2, keep=root)
    )
    own = jnp.where(x == 0, quarter[0], from_root)
    own = jnp.where(low == 0, own, shifted(own, low=1, keep=plane))
    after = shifted(own, x=-1, keep=lane)
    before = shifted(own, x=1, keep=lane)
    across = shifted(own, x=2, keep=lane)
    return [own, after, across, before]


def shards(right_sides, panel_diag, left_factor, right_factor, tile_scale, tile_rank):
    rows, _ = right_sides.shape
    count = rows // SIZE
    row = lax.axis_index("row")
    col = lax.axis_index("rhs")
    x, low, core = row // 4, (row // 2) % 2, row % 2
    y, high = col // 2, col % 2
    place = jnp.stack([x, low, core, y, high, row]).astype(jnp.int32)

    left_lanes = jnp.transpose(right_factor, (1, 2, 0)).reshape(TILE, count, 4, TILE)
    left_lanes = jnp.transpose(left_lanes, (1, 2, 0, 3)).reshape(count, SIZE, TILE)
    packed = jnp.concatenate([left_lanes, left_factor.reshape(count, SIZE, TILE)], axis=1)

    def lone(factor):
        return jnp.transpose(
            jnp.transpose(factor[:SIZE, 0, :], (1, 0)).reshape(64, 4, TILE), (1, 0, 2)
        ).reshape(256, TILE)

    tile = jnp.concatenate([lone(right_factor), lone(left_factor)], axis=0)
    solver = lambda a, b, c: a == 0 and b == 0 and c == 1
    tile = jnp.concatenate([tile, shifted(tile, high=1, keep=solver)], axis=0)
    turns = (1, 3, 2)
    tiles = [tile] + [shifted(tile, y=dy, keep=solver) for dy in turns]
    tile_places = [((4 - dy) % 4, dh) for dy in (0, *turns) for dh in (0, 1)]

    up = shifted(packed, y=1)
    down = shifted(packed, y=-1)
    over = shifted(packed, high=1)
    over_up = shifted(over, y=1)
    over_down = shifted(over, y=-1)
    far = shifted(up, y=1)
    over_far = shifted(over_down, y=-1)
    pieces = [packed, up, down, over, over_up, over_down, far, over_far]
    places = [(0, 0), (3, 0), (1, 0), (0, 1), (3, 1), (1, 1), (2, 0), (2, 1)]

    *right, right_whole = root_copies(place, right_sides)
    near = shifted(right_whole, core=1, keep=lambda a, b, c: a == 0 and b == 0 and c == 0)
    inverse = inverses(panel_diag)
    scalars = (place, tile_scale.T, tile_rank.T)
    first = first_solution(place, inverse, spread(0, right, x, low))
    first_core = shifted(first, core=1)
    middle = update(0, scalars, places, right_sides, pieces, [first, first_core])
    quarters = second_solution(scalars, tile_places, inverse, near, right_sides, tiles)
    second = spread(1, quarters, x, low)
    second_core = [shifted(quarter, core=1) for quarter in second]
    return update(1, scalars, places, middle, pieces, second + second_core)


def solution(mesh):
    placed = (
        P("row", "rhs"),
        P(),
        P("row", None, "rhs"),
        P("row", None, "rhs"),
        P("row", None),
        P("row", None),
    )
    return jax.shard_map(shards, mesh=mesh, in_specs=placed, out_specs=P("row", "rhs"), check_vma=False)
```
